256 devices in a mesh: segment: 8 (over y, core), dp: 32 (over z, x).
Axes of the slice: x: 4, y: 4, z: 8, core: 2. Of those that a mesh axis runs over, the one named last changes fastest.
Arguments:
- student_in: bfloat16 [4, 64, 8, 8, 512], P(None, 'dp'), may hold values from -6 to 6
- teacher_in: bfloat16 [4, 64, 8, 8, 512], P(None, 'dp'), may hold values from -6 to 6
- out_grad: bfloat16 [4, 64, 8, 8, 512], P(None, 'dp'), may hold values from -6 to 6
- student_params: float32 [8, 2621440], P('segment', 'dp'), may hold values from -0.5625 to 0.5625, as said below
- teacher_params: float32 [8, 2621440], P('segment', 'dp'), may hold values from -0.5625 to 0.5625, as said below
Outputs:
- teacher_acts: bfloat16 [8, 4, 64, 8, 8, 512], P('segment', None, 'dp')
- input_grads: bfloat16 [8, 4, 64, 8, 8, 512], P('segment', None, 'dp')
- param_grads: float32 [8, 2621440], P('segment', 'dp')
- teacher_new: float32 [8, 2621440], P('segment', 'dp')
The draws below stay inside these ranges and needn't reach their ends.
Inputs may be any that keep to these rules, and one draw needn't show every extreme that they name: `student_params`: independent entries of both signs. `teacher_params`: independent entries of both signs.
All inputs are finite; a program needn't handle non-finite values.
Results may differ from the reference program's by a relative error of at most 0.03.
Values may be sent and summed in bfloat16 or wider, within the bound.
No kernel may reach another device: no remote copies, remote signals or barrier semaphores. Data moves between devices by JAX's collectives and lax.ppermute only.
A program may use at most 128 MiB of HBM per device.

```python
import jax
import jax.numpy as jnp
from jax import lax

C = 512
SE = 256
SIDE = 8
MICRO = 4
L = 8
IMGS = 64
PARAMS = 2621440


def param_rows(key):
    position = jnp.arange(PARAMS)
    tap_count = 9 * C * C
    scale = jnp.where(position < tap_count, (9.0 * C) ** (-0.5), jnp.where(position < tap_count + C * SE, 2.0 * C ** (-0.5), 3.0 * SE ** (-0.5)))
    base = jax.random.truncated_normal(key, -3.0, 3.0, (L, PARAMS), jnp.float32)
    return base * scale[None, :]


def draw_student_params(key, part):
    return param_rows(jax.random.fold_in(key, 11))


def draw_teacher_params(key, part):
    return param_rows(jax.random.fold_in(key, 23))


def levels(own_key, shape, pieces, low, top_value):
    factor_of = 1.0
    for dim, shards_of in pieces:
        draws = jax.random.uniform(jax.random.fold_in(jax.random.fold_in(own_key, 6), dim), (shards_of,), jnp.float32, low / len(pieces), top_value / len(pieces))
        factor_of = factor_of * jnp.repeat(jnp.exp(draws), shape[dim] // shards_of).reshape((-1,) + (1,) * (len(shape) - 1 - dim))
    return factor_of


def normal_values(rng, shape, width, bound, pieces=(), kind=jnp.bfloat16):
    values = width * jax.random.normal(rng, shape, jnp.float32)
    if pieces:
        values = values * levels(rng, shape, pieces, -0.22, 0.18)
    return jnp.clip(values, -bound, bound).astype(kind)


def setup_inputs(seed: int = 0) -> dict:
    seeds = jax.random.split(jax.random.key(seed), 6)
    student_in = normal_values(seeds[0], (MICRO, IMGS, SIDE, SIDE, C), 1.0, 6.0, ((1, 32),))
    teacher_in = normal_values(seeds[1], (MICRO, IMGS, SIDE, SIDE, C), 1.0, 6.0, ((1, 32),))
    out_grad = normal_values(seeds[2], (MICRO, IMGS, SIDE, SIDE, C), 1.0, 6.0, ((1, 32),))
    student_params = draw_student_params(jax.random.fold_in(seeds[5], 71), 0)
    teacher_params = draw_teacher_params(jax.random.fold_in(seeds[5], 71), 0)
    return {"student_in": student_in, "teacher_in": teacher_in, "out_grad": out_grad, "student_params": student_params, "teacher_params": teacher_params}


ema_keep = 0.99
step_rate = 0.001

def split_row(row, channels, squeeze):
    tap_count = 9 * channels * channels
    kernel = row[:tap_count].reshape(9 * channels, channels)
    reduce_w = row[tap_count:tap_count + channels * squeeze].reshape(channels, squeeze)
    expand_w = row[tap_count + channels * squeeze:].reshape(squeeze, channels)
    return (kernel, reduce_w, expand_w)

def gated_block(images, kernel, reduce_w, expand_w):
    side_h, side_w, channels = (images.shape[1], images.shape[2], images.shape[3])
    padded = jnp.pad(images, ((0, 0), (1, 1), (1, 1), (0, 0)))
    columns = jnp.concatenate([padded[:, row_off:row_off + side_h, col_off:col_off + side_w, :] for row_off in range(3) for col_off in range(3)], axis=-1)
    mixed_sum = jnp.dot(columns.reshape(-1, 9 * channels), kernel, preferred_element_type=jnp.float32)
    active = jax.nn.silu(mixed_sum).reshape(images.shape)
    pooled = lax.optimization_barrier(jnp.mean(active, axis=(1, 2))).astype(jnp.bfloat16)
    hidden = jax.nn.silu(jnp.dot(pooled, reduce_w, preferred_element_type=jnp.float32)).astype(jnp.bfloat16)
    gate_val = jax.nn.sigmoid(jnp.dot(hidden, expand_w, preferred_element_type=jnp.float32))
    return (images.astype(jnp.float32) + active * gate_val[:, None, None, :]).astype(jnp.bfloat16)

def one_image(picture, kernel, reduce_w, expand_w, cotangent):

    def local_block(inputs_one, kern_one, red_one, exp_one):
        return gated_block(inputs_one[None], kern_one, red_one, exp_one)[0]
    primal_out, pull_back = jax.vjp(local_block, picture, kernel, reduce_w, expand_w)
    return pull_back(cotangent.astype(primal_out.dtype))

def reference(student_in, teacher_in, out_grad, student_params, teacher_params):
    student_in = student_in.astype(jnp.bfloat16)
    teacher_in = teacher_in.astype(jnp.bfloat16)
    out_grad = out_grad.astype(jnp.bfloat16)
    student_params = student_params.astype(jnp.float32)
    teacher_params = teacher_params.astype(jnp.float32)
    micro_count, image_count = (student_in.shape[0], student_in.shape[1])
    channels = student_in.shape[-1]
    flat_shape = (micro_count * image_count,) + student_in.shape[2:]
    current = student_in
    teacher_now = teacher_in
    saved = []
    teacher_list = []
    weights_list = []
    for layer_idx in range(L):
        student_w = split_row(student_params[layer_idx].astype(jnp.bfloat16), channels, SE)
        teacher_w = split_row(teacher_params[layer_idx].astype(jnp.bfloat16), channels, SE)
        weights_list.append(student_w)
        saved.append(current)
        current = lax.map(lambda group: gated_block(group, *student_w), current)
        teacher_now = lax.map(lambda group: gated_block(group, *teacher_w), teacher_now)
        teacher_list.append(teacher_now)
    cotangent = out_grad.reshape(flat_shape)
    grads_list = [None] * L
    rows_list = [None] * L
    for layer_idx in range(L - 1, -1, -1):
        kernel, reduce_w, expand_w = weights_list[layer_idx]

        def per_image(totals, inputs_pair):
            picture, cot_one = inputs_pair
            d_in, d_kern, d_red, d_exp = one_image(picture, kernel, reduce_w, expand_w, cot_one)
            return ((totals[0] + d_kern.astype(jnp.float32), totals[1] + d_red.astype(jnp.float32), totals[2] + d_exp.astype(jnp.float32)), d_in.astype(jnp.bfloat16))
        zero_sums = (jnp.zeros(kernel.shape, jnp.float32), jnp.zeros(reduce_w.shape, jnp.float32), jnp.zeros(expand_w.shape, jnp.float32))
        totals, cotangent = lax.scan(per_image, zero_sums, (saved[layer_idx].reshape(flat_shape), cotangent))
        grads_list[layer_idx] = cotangent.reshape(student_in.shape)
        rows_list[layer_idx] = jnp.concatenate([totals[0].reshape(-1), totals[1].reshape(-1), totals[2].reshape(-1)])
    param_grads = jnp.stack(rows_list)
    teacher_new = ema_keep * teacher_params + (1.0 - ema_keep) * (student_params - step_rate * param_grads)
    return (jnp.stack(teacher_list), jnp.stack(grads_list), param_grads, teacher_new)
```

```python
import jax
import jax.numpy as jnp
import numpy as np
from jax import lax
from jax.experimental import pallas as pl
from jax.experimental.pallas import tpu as pltpu
from jax.sharding import Mesh, PartitionSpec as P

C = 512
SE = 256
SIDE = 8
TAPS = 9 * C
ROWS = TAPS + 2 * SE
HIGH = TAPS // 3

ema_keep = 0.99
step_rate = 0.001

f32 = jnp.float32
bf16 = jnp.bfloat16


def mm(a, b):
    return jnp.dot(a, b, preferred_element_type=f32)


def mm_t(a, b):
    return lax.dot_general(a, b, (((1,), (1,)), ((), ())), preferred_element_type=f32)


def selector(odd):
    channel = lax.broadcasted_iota(jnp.int32, (C, SE), 0)
    half = lax.broadcasted_iota(jnp.int32, (C, SE), 1)
    return jnp.where(channel == 2 * half + odd, 1.0, 0.0).astype(bf16)


def put_shifted(values, store, images):
    pad = images * SIDE
    count = SIDE * pad
    tiles = values.reshape(count // 8, 8, C)
    column = lax.broadcasted_iota(jnp.int32, (count // 8, 8, C), 1)
    left = jnp.where(column == 0, 0.0, pltpu.roll(tiles, 1, 1))
    right = jnp.where(column == 7, 0.0, pltpu.roll(tiles, 7, 1))
    store[0:pad, :] = jnp.zeros((pad, 3 * C), bf16)
    store[pad + count :, :] = jnp.zeros((pad, 3 * C), bf16)
    store[pad : pad + count, 0:C] = left.reshape(count, C).astype(bf16)
    store[pad : pad + count, C : 2 * C] = values.astype(bf16)
    store[pad : pad + count, 2 * C :] = right.reshape(count, C).astype(bf16)


def weight_copies(w_refs, w_store, sems):
    found = []
    for layer, w_ref in enumerate(w_refs):
        pieces = []
        for piece in range(4):
            start = piece * HIGH
            size = HIGH if piece < 3 else ROWS - TAPS
            pieces.append(
                pltpu.make_async_copy(
                    w_ref.at[pl.ds(start, size), :],
                    w_store.at[layer, pl.ds(start, size), :],
                    sems.at[layer, piece],
                )
            )
        found.append(pieces)
    return found


def spread(per_image, images):
    return jnp.broadcast_to(per_image.reshape(1, images, 1, C), (SIDE, images, SIDE, C)).reshape(
        SIDE * images * SIDE, C
    )


def image_sum(values, images):
    return jnp.sum(jnp.sum(values.reshape(SIDE, images, SIDE, C), axis=0), axis=1)


def layer_forward(x, layer, copies, w_store, x_store, images):
    count = SIDE * images * SIDE
    put_shifted(x, x_store, images)
    mixed = None
    for high in range(3):
        copies[high].wait()
        part = mm(
            x_store[high * images * SIDE : high * images * SIDE + count, :],
            w_store[layer, high * HIGH : (high + 1) * HIGH, :],
        )
        mixed = part if mixed is None else mixed + part
    active = mixed * jax.nn.sigmoid(mixed)
    pooled = (image_sum(active, images) * (1.0 / (SIDE * SIDE))).astype(bf16)
    copies[3].wait()
    reduce_w = w_store[layer, TAPS : TAPS + SE, :]
    expand_w = w_store[layer, TAPS + SE : ROWS, :]
    even = mm(pooled, selector(0)).astype(bf16)
    odd = mm(pooled, selector(1)).astype(bf16)
    before = mm(even, reduce_w[:, :SE]) + mm(odd, reduce_w[:, SE:])
    hidden = (before * jax.nn.sigmoid(before)).astype(bf16)
    gate = jax.nn.sigmoid(mm(hidden, expand_w))
    out = x + active * spread(gate, images)
    return out.astype(bf16), mixed, pooled, before, gate


def forward_stage(images, keep):
    count = SIDE * images * SIDE

    def body(on, x_ref, w0, w1, mid_ref, out_ref, *rest):
        saved = rest[:-3]
        w_store, x_store, sems = rest[-3:]

        @pl.when(on[0] == 1)
        def _():
            copies = weight_copies((w0, w1), w_store, sems)
            for pieces in copies:
                for piece in pieces:
                    piece.start()
            x = x_ref[...].astype(f32)
            for layer in range(2):
                out, mixed, pooled, before, gate = layer_forward(
                    x, layer, copies[layer], w_store, x_store, images
                )
                (mid_ref, out_ref)[layer][...] = out
                if keep:
                    mixed_ref, pooled_ref, before_ref, gate_ref = saved
                    mixed_ref[layer] = mixed
                    pooled_ref[layer] = pooled.astype(f32)
                    before_ref[layer] = before
                    gate_ref[layer] = gate
                x = out.astype(f32)

    shapes = [jax.ShapeDtypeStruct((count, C), bf16)] * 2
    if keep:
        shapes += [
            jax.ShapeDtypeStruct((2, count, C), f32),
            jax.ShapeDtypeStruct((2, images, C), f32),
            jax.ShapeDtypeStruct((2, images, SE), f32),
            jax.ShapeDtypeStruct((2, images, C), f32),
        ]
    vmem = pl.BlockSpec(memory_space=pltpu.VMEM)
    hbm = pl.BlockSpec(memory_space=pl.ANY)
    return pl.pallas_call(
        body,
        out_shape=shapes,
        in_specs=[pl.BlockSpec(memory_space=pltpu.SMEM), vmem, hbm, hbm],
        out_specs=[vmem] * len(shapes),
        scratch_shapes=[
            pltpu.VMEM((2, ROWS, C), bf16),
            pltpu.VMEM((count + 2 * images * SIDE, 3 * C), bf16),
            pltpu.SemaphoreType.DMA((2, 4)),
        ],
        compiler_params=pltpu.CompilerParams(vmem_limit_bytes=40 * 1024 * 1024),
        name="forward_stage",
    )


def layer_backward(dy, layer, copies, w_store, d_store, mixed, before, gate, images):
    count = SIDE * images * SIDE
    sig = jax.nn.sigmoid(mixed)
    active = mixed * sig
    d_gate = image_sum(dy * active, images)
    d_logit = d_gate * gate * (1.0 - gate)
    copies[3].wait()
    reduce_w = w_store[layer, TAPS : TAPS + SE, :]
    expand_w = w_store[layer, TAPS + SE : ROWS, :]
    d_hidden = mm_t(d_logit.astype(bf16), expand_w).astype(bf16).astype(f32)
    soft = jax.nn.sigmoid(before)
    d_before = d_hidden * (soft + before * soft * (1.0 - soft))
    low = d_before.astype(bf16)
    d_even = mm_t(low, reduce_w[:, :SE]).astype(bf16)
    d_odd = mm_t(low, reduce_w[:, SE:]).astype(bf16)
    d_pooled = mm_t(d_even, selector(0)) + mm_t(d_odd, selector(1))
    d_active = dy * spread(gate, images) + spread(d_pooled * (1.0 / (SIDE * SIDE)), images)
    d_mixed = d_active * (sig + active * (1.0 - sig))
    put_shifted(d_mixed, d_store, images)
    dx = dy
    for high in range(3):
        copies[high].wait()
        rows = slice((2 - high) * images * SIDE, (2 - high) * images * SIDE + count)
        for side in range(3):
            tap = 3 * high + side
            dx = dx + mm_t(
                d_store[rows, (2 - side) * C : (3 - side) * C],
                w_store[layer, tap * C : (tap + 1) * C, :],
            )
    return dx.astype(bf16), d_mixed.astype(bf16), d_logit, d_before


def backward_stage(images):
    count = SIDE * images * SIDE

    def body(on, dy_ref, mixed_ref, pooled_ref, before_ref, gate_ref, w0, w1, dx_ref, d_ref, se_ref, w_store, d_store, sems):
        @pl.when(on[0] == 1)
        def _():
            copies = weight_copies((w0, w1), w_store, sems)
            for layer in (1, 0):
                for piece in (3, 0, 1, 2):
                    copies[layer][piece].start()
            dy = dy_ref[...].astype(f32)
            for layer in (1, 0):
                before = before_ref[layer]
                dx, d_mixed, d_logit, d_before = layer_backward(
                    dy, layer, copies[layer], w_store, d_store,
                    mixed_ref[layer], before, gate_ref[layer], images,
                )
                dx_ref[layer] = dx
                d_ref[layer] = d_mixed
                hidden = before * jax.nn.sigmoid(before)
                se_ref[layer, 0] = pooled_ref[layer]
                se_ref[layer, 1] = d_logit
                se_ref[layer, 2, :, :SE] = hidden
                se_ref[layer, 2, :, SE:] = d_before
                dy = dx.astype(f32)

    vmem = pl.BlockSpec(memory_space=pltpu.VMEM)
    hbm = pl.BlockSpec(memory_space=pl.ANY)
    return pl.pallas_call(
        body,
        out_shape=[
            jax.ShapeDtypeStruct((2, count, C), bf16),
            jax.ShapeDtypeStruct((2, count, C), bf16),
            jax.ShapeDtypeStruct((2, 3, images, C), f32),
        ],
        in_specs=[pl.BlockSpec(memory_space=pltpu.SMEM)] + [vmem] * 5 + [hbm] * 2,
        out_specs=[vmem] * 3,
        scratch_shapes=[
            pltpu.VMEM((2, ROWS, C), bf16),
            pltpu.VMEM((count + 2 * images * SIDE, 3 * C), bf16),
            pltpu.SemaphoreType.DMA((2, 4)),
        ],
        compiler_params=pltpu.CompilerParams(vmem_limit_bytes=40 * 1024 * 1024),
        name="backward_stage",
    )


def weight_grad(images, dp_z, dp_x):
    count = SIDE * images * SIDE
    part = ROWS // (dp_z * dp_x)
    last = (dp_z - 1) * dp_x * part
    tall = TAPS - last

    def body(place, x_ref, d_ref, se_ref, out_ref, x_store, left_store, se_store):
        @pl.when(place[0] >= 0)
        def _():
            put_shifted(x_ref[...].astype(f32), x_store, images)
            for high in range(3):
                for side in range(3):
                    tap = 3 * high + side
                    rows = slice(high * images * SIDE, high * images * SIDE + count)
                    left_store[tap * C : (tap + 1) * C, :] = x_store[rows, side * C : (side + 1) * C].T
            left_store[TAPS:, :] = jnp.zeros((ROWS - TAPS, count), bf16)
            pooled = se_ref[0]
            d_logit = se_ref[1]
            hidden = se_ref[2, :, :SE]
            d_before = se_ref[2, :, SE:]

            def outer(a, b):
                return lax.dot_general(a.astype(bf16), b.astype(bf16), (((0,), (0,)), ((), ())), preferred_element_type=f32)

            even = mm(pooled.astype(bf16), selector(0))
            odd = mm(pooled.astype(bf16), selector(1))
            se_store[0:tall, :] = jnp.zeros((tall, C), f32)
            se_store[tall : tall + SE, 0:SE] = outer(even, d_before)
            se_store[tall : tall + SE, SE:] = outer(odd, d_before)
            se_store[tall + SE :, :] = outer(hidden, d_logit)
            for z in range(dp_z):
                begin = pl.multiple_of(z * dp_x * part + place[0] * part, 32)
                block = mm(left_store[pl.ds(begin, part), :], d_ref[...])
                if z == dp_z - 1:
                    block = block + se_store[pl.ds(pl.multiple_of(place[0] * part, 32), part), :]
                out_ref[z * part : (z + 1) * part, :] = block.astype(bf16)

    vmem = pl.BlockSpec(memory_space=pltpu.VMEM)
    return pl.pallas_call(
        body,
        out_shape=jax.ShapeDtypeStruct((dp_z * part, C), bf16),
        in_specs=[pl.BlockSpec(memory_space=pltpu.SMEM)] + [vmem] * 3,
        out_specs=vmem,
        scratch_shapes=[
            pltpu.VMEM((count + 2 * images * SIDE, 3 * C), bf16),
            pltpu.VMEM((ROWS, count), bf16),
            pltpu.VMEM((ROWS - last, C), f32),
        ],
        compiler_params=pltpu.CompilerParams(vmem_limit_bytes=56 * 1024 * 1024),
        name="weight_grad",
    )


def swap(value):
    return lax.ppermute(value, "core", [(0, 1), (1, 0)])


def per_device(student_in, teacher_in, out_grad, student_params, teacher_params):
    micro = student_in.shape[0]
    stages = lax.axis_size("y")
    dp_z = lax.axis_size("z")
    dp_x = lax.axis_size("x")
    y = lax.axis_index("y")
    core = lax.axis_index("core")
    first_core = core == 0
    images = micro
    count = SIDE * images * SIDE

    def own(array):
        taken = lax.dynamic_index_in_dim(array, core, 1, keepdims=False)
        return taken.transpose(1, 0, 2, 3).reshape(count, C)

    def gathered(row):
        mat = row.astype(bf16).reshape(-1, C)
        return lax.all_gather(lax.all_gather(mat, "x", axis=0, tiled=True), "z", axis=0, tiled=True)

    def both(weights):
        other = swap(weights)
        return (
            jnp.where(first_core, weights, other),
            jnp.where(first_core, other, weights),
        )

    def on(stage):
        return (y == stage).astype(jnp.int32).reshape(1)

    forward = [(i, i + 1) for i in range(stages - 1)]
    back = [(i + 1, i) for i in range(stages - 1)]

    student_w = gathered(student_params)
    s0, s1 = both(student_w)
    teacher_row, _ = lax.optimization_barrier((teacher_params, student_w))
    teacher_w = gathered(teacher_row)

    run = forward_stage(images, True)
    now = own(student_in)
    kept = []
    for stage in range(stages):
        mid, out, *saved = run(on(stage), now, s0, s1)
        kept.append((now, mid, saved))
        if stage + 1 < stages:
            now = lax.ppermute(out, "y", forward)

    run_back = backward_stage(images)
    now = own(out_grad)
    dx = d_mixed = se = x_in = None

    def pick(stage, new, old):
        return new if old is None else jax.tree.map(lambda a, b: jnp.where(y == stage, a, b), new, old)

    for stage in range(stages - 1, -1, -1):
        x0, x1, saved = kept[stage]
        new_dx, new_d, new_se = run_back(on(stage), now, *saved, s0, s1)
        dx, d_mixed, se, x_in = pick(stage, (new_dx, new_d, new_se, (x0, x1)), None if dx is None else (dx, d_mixed, se, x_in))
        if stage > 0:
            now = lax.ppermute(new_dx[0], "y", back)

    t0, t1 = both(teacher_w)
    run_teacher = forward_stage(images, False)
    now = own(teacher_in)
    acts = None
    for stage in range(stages):
        mid, out = run_teacher(on(stage), now, t0, t1)
        acts = pick(stage, (mid, out), acts)
        if stage + 1 < stages:
            now = lax.ppermute(out, "y", forward)

    def trade(pair):
        mine = jnp.where(first_core, pair[0], pair[1])
        theirs = swap(jnp.where(first_core, pair[1], pair[0]))
        return mine, theirs

    def placed(pair):
        mine, theirs = trade(pair)
        ordered = jnp.stack((jnp.where(first_core, mine, theirs), jnp.where(first_core, theirs, mine)))
        return ordered.reshape(2, SIDE, micro, SIDE, C).transpose(2, 0, 1, 3, 4)[None]

    def grouped(pair, fixed):
        mine, theirs = trade(pair)
        pieces = jnp.stack((mine, theirs))
        pieces = lax.all_gather(pieces, "x", axis=0, tiled=True)
        return pieces

    group = 2 * dp_x
    x_all = grouped(x_in, None)
    d_all = grouped((d_mixed[0], d_mixed[1]), None)
    se_all = grouped((se[0].astype(bf16), se[1].astype(bf16)), None)

    def as_rows(pieces):
        shaped = pieces.reshape(group, SIDE, images, SIDE, C).transpose(1, 0, 2, 3, 4)
        return shaped.reshape(SIDE * group * images * SIDE, C)

    se_rows = se_all.astype(f32).transpose(1, 0, 2, 3).reshape(3, group * images, C)
    place = lax.axis_index("x").astype(jnp.int32).reshape(1)
    blocks = weight_grad(group * images, dp_z, dp_x)(place, as_rows(x_all), as_rows(d_all), se_rows)
    shard = lax.psum_scatter(blocks, "z", scatter_dimension=0, tiled=True)
    grad = shard.astype(f32).reshape(1, -1)
    teacher_new = ema_keep * teacher_params + (1.0 - ema_keep) * (student_params - step_rate * grad)
    return placed(acts), placed((dx[0], dx[1])), grad, teacher_new


def solution(mesh):
    grid = Mesh(mesh.devices.reshape(4, 2, 8, 4), ("y", "core", "z", "x"))
    seg = ("y", "core")
    dp = ("z", "x")
    image_spec = P(None, dp, None, None, None)
    return jax.shard_map(
        per_device,
        mesh=grid,
        in_specs=(image_spec, image_spec, image_spec, P(seg, dp), P(seg, dp)),
        out_specs=(
            P(seg, None, dp, None, None, None),
            P(seg, None, dp, None, None, None),
            P(seg, dp),
            P(seg, dp),
        ),
        check_vma=False,
    )
```

```python
import jax
import jax.numpy as jnp
import numpy as np
from jax import lax
from jax.experimental import pallas as pl
from jax.experimental.pallas import tpu as pltpu
from jax.sharding import Mesh, PartitionSpec as P

C = 512
SE = 256
SIDE = 8
TAPS = 9 * C
ROWS = TAPS + 2 * SE
HIGH = TAPS // 3
EXTRA = 32
MIB = 1024 * 1024

ema_keep = 0.99
step_rate = 0.001

f32 = jnp.float32
bf16 = jnp.bfloat16


def mm(a, b):
    return jnp.dot(a, b, preferred_element_type=f32)


def mm_t(a, b):
    return lax.dot_general(a, b, (((1,), (1,)), ((), ())), preferred_element_type=f32)


def selector(odd):
    channel = lax.broadcasted_iota(jnp.int32, (C, SE), 0)
    half = lax.broadcasted_iota(jnp.int32, (C, SE), 1)
    return jnp.where(channel == 2 * half + odd, 1.0, 0.0).astype(bf16)


def put_shifted(values, store, images):
    pad = images * SIDE
    count = SIDE * pad
    tiles = values.reshape(count // 8, 8, C)
    column = lax.broadcasted_iota(jnp.int32, (count // 8, 8, C), 1)
    left = jnp.where(column == 0, 0.0, pltpu.roll(tiles, 1, 1))
    right = jnp.where(column == 7, 0.0, pltpu.roll(tiles, 7, 1))
    store[0:pad, :] = jnp.zeros((pad, 3 * C), bf16)
    store[pad + count :, :] = jnp.zeros((pad, 3 * C), bf16)
    store[pad : pad + count, 0:C] = left.reshape(count, C).astype(bf16)
    store[pad : pad + count, C : 2 * C] = values.astype(bf16)
    store[pad : pad + count, 2 * C :] = right.reshape(count, C).astype(bf16)


def piece_spots(place, sizes):
    z, dp_z, rows = place[2], len(sizes) - 1, sizes[0]
    spots = [z * rows]
    for step in range(1, dp_z // 2 + 1):
        spots.append(((z + dp_z - step) % dp_z) * rows)
        high = ((z + step) % dp_z) * rows
        spots.append(high + rows // 2 if step == dp_z // 2 else high)
    return spots


class Weights:
    def __init__(self, place, own, other, store, sems, groups):
        core = place[1]
        rows = ROWS // groups
        self.store, self.sems, self.groups = store, sems, groups
        self.whole = own[0] if own[0].shape[0] == rows else own[0].at[pl.ds(0, rows), :]
        self.core = core
        self.lists = []
        for refs, slot in ((own, core), (other, 1 - core)):
            found = []
            if len(refs) == 1:
                for z in range(groups):
                    found.append(
                        pltpu.make_async_copy(
                            refs[0].at[pl.ds(z * rows, rows), :],
                            store.at[slot, pl.ds(z * rows, rows), :],
                            sems.at[slot, z],
                        )
                    )
            else:
                sizes = [ref.shape[0] for ref in refs]
                for ref, spot in zip(refs, piece_spots(place, sizes)):
                    spot = pl.multiple_of(spot, 64)
                    found.append(
                        pltpu.make_async_copy(
                            ref, store.at[slot, pl.ds(spot, ref.shape[0]), :], sems.at[slot, spot // rows]
                        )
                    )
            self.lists.append(found)

    def start(self, first):
        own, other = self.lists

        @pl.when(self.core == first)
        def _():
            for copy in own + other:
                copy.start()

        @pl.when(self.core != first)
        def _():
            for copy in other + own:
                copy.start()

    def wait(self, layer, begin, end):
        rows = ROWS // self.groups
        for z in range(begin, end):
            pltpu.make_async_copy(
                self.whole, self.store.at[layer, pl.ds(z * rows, rows), :], self.sems.at[layer, z]
            ).wait()

    def need(self, layer, high):
        rows = ROWS // self.groups
        begin = 0 if high == 0 else -(-high * HIGH // rows)
        end = self.groups if high == 2 else -(-(high + 1) * HIGH // rows)
        self.wait(layer, begin, end)


def spread(per_image, images):
    return jnp.broadcast_to(per_image.reshape(1, images, 1, C), (SIDE, images, SIDE, C)).reshape(
        SIDE * images * SIDE, C
    )


def image_sum(values, images):
    return jnp.sum(jnp.sum(values.reshape(SIDE, images, SIDE, C), axis=0), axis=1)


def assemble(pieces, groups):
    def body(place, *rest):
        own, other = rest[:pieces], rest[pieces : 2 * pieces]
        out_ref, sems = rest[2 * pieces :]
        weights = Weights(place, own, other, out_ref, sems, groups)
        weights.start(0)
        for layer in range(2):
            weights.wait(layer, 0, groups)

    return pl.pallas_call(
        body,
        out_shape=pltpu.VMEM((2, ROWS, C), bf16),
        in_specs=[pl.BlockSpec(memory_space=pltpu.SMEM)]
        + [pl.BlockSpec(memory_space=pltpu.HBM)] * (2 * pieces),
        out_specs=pl.BlockSpec(memory_space=pltpu.VMEM),
        scratch_shapes=[pltpu.SemaphoreType.DMA((2, groups))],
        compiler_params=pltpu.CompilerParams(vmem_limit_bytes=12 * MIB),
        name="assemble",
    )


class Resident:
    groups = 0

    def need(self, layer, high):
        pass

    def wait(self, layer, begin, end):
        pass


def layer_forward(x, layer, weights, w_store, x_store, images):
    count = SIDE * images * SIDE
    put_shifted(x, x_store, images)
    mixed = None
    for high in range(3):
        weights.need(layer, high)
        part = mm(
            x_store[high * images * SIDE : high * images * SIDE + count, :],
            w_store[layer, high * HIGH : (high + 1) * HIGH, :],
        )
        mixed = part if mixed is None else mixed + part
    active = mixed * jax.nn.sigmoid(mixed)
    pooled = (image_sum(active, images) * (1.0 / (SIDE * SIDE))).astype(bf16)
    reduce_w = w_store[layer, TAPS : TAPS + SE, :]
    expand_w = w_store[layer, TAPS + SE : ROWS, :]
    even = mm(pooled, selector(0)).astype(bf16)
    odd = mm(pooled, selector(1)).astype(bf16)
    before = mm(even, reduce_w[:, :SE]) + mm(odd, reduce_w[:, SE:])
    hidden = (before * jax.nn.sigmoid(before)).astype(bf16)
    gate = jax.nn.sigmoid(mm(hidden, expand_w))
    out = x + active * spread(gate, images)
    return out.astype(bf16), mixed, pooled, before, gate


def stage_specs(vmem_inputs, pieces):
    return (
        [pl.BlockSpec(memory_space=pltpu.SMEM)]
        + [pl.BlockSpec(memory_space=pltpu.VMEM)] * vmem_inputs
        + [pl.BlockSpec(memory_space=pltpu.HBM)] * (2 * pieces)
    )


def shift_scratch(images):
    return [pltpu.VMEM(((SIDE + 2) * images * SIDE, 3 * C), bf16)]


def store_scratch(groups):
    return [pltpu.VMEM((2, ROWS, C), bf16), pltpu.SemaphoreType.DMA((2, groups))]


def forward_stage(stage, images, pieces, groups, keep):
    count = SIDE * images * SIDE

    def body(place, x_ref, *rest):
        if keep:
            w_store, mid_ref, out_ref, *saved = rest[:-1]
            x_store = rest[-1]
        else:
            own, other = rest[:pieces], rest[pieces : 2 * pieces]
            mid_ref, out_ref, *saved = rest[2 * pieces : -3]
            x_store, w_store, sems = rest[-3:]

        @pl.when(place[0] == stage)
        def _():
            if keep:
                weights = Resident()
            else:
                weights = Weights(place, own, other, w_store, sems, groups)
                weights.start(0)
            x = x_ref[...].astype(f32)
            for layer in range(2):
                out, mixed, pooled, before, gate = layer_forward(
                    x, layer, weights, w_store, x_store, images
                )
                (mid_ref, out_ref)[layer][...] = out
                if keep:
                    mixed_ref, pooled_ref, before_ref, gate_ref = saved
                    mixed_ref[layer] = mixed
                    pooled_ref[layer] = pooled.astype(f32)
                    before_ref[layer] = before
                    gate_ref[layer] = gate
                x = out.astype(f32)

    shapes = [jax.ShapeDtypeStruct((count, C), bf16)] * 2
    if keep:
        shapes += [
            jax.ShapeDtypeStruct((2, count, C), f32),
            jax.ShapeDtypeStruct((2, images, C), f32),
            jax.ShapeDtypeStruct((2, images, SE), f32),
            jax.ShapeDtypeStruct((2, images, C), f32),
        ]
    return pl.pallas_call(
        body,
        out_shape=shapes,
        in_specs=stage_specs(2, 0) if keep else stage_specs(1, pieces),
        out_specs=[pl.BlockSpec(memory_space=pltpu.VMEM)] * len(shapes),
        scratch_shapes=shift_scratch(images) + ([] if keep else store_scratch(groups)),
        compiler_params=pltpu.CompilerParams(vmem_limit_bytes=(14 if keep else 24) * MIB),
        name="forward_stage",
    )


def layer_backward(dy, layer, weights, w_store, d_store, mixed, before, gate, images):
    count = SIDE * images * SIDE
    sig = jax.nn.sigmoid(mixed)
    active = mixed * sig
    d_gate = image_sum(dy * active, images)
    d_logit = d_gate * gate * (1.0 - gate)
    weights.wait(layer, 0, weights.groups)
    reduce_w = w_store[layer, TAPS : TAPS + SE, :]
    expand_w = w_store[layer, TAPS + SE : ROWS, :]
    d_hidden = mm_t(d_logit.astype(bf16), expand_w).astype(bf16).astype(f32)
    soft = jax.nn.sigmoid(before)
    d_before = d_hidden * (soft + before * soft * (1.0 - soft))
    low = d_before.astype(bf16)
    d_even = mm_t(low, reduce_w[:, :SE]).astype(bf16)
    d_odd = mm_t(low, reduce_w[:, SE:]).astype(bf16)
    d_pooled = mm_t(d_even, selector(0)) + mm_t(d_odd, selector(1))
    d_active = dy * spread(gate, images) + spread(d_pooled * (1.0 / (SIDE * SIDE)), images)
    d_mixed = d_active * (sig + active * (1.0 - sig))
    put_shifted(d_mixed, d_store, images)
    dx = dy
    for high in range(3):
        rows = slice((2 - high) * images * SIDE, (2 - high) * images * SIDE + count)
        for side in range(3):
            tap = 3 * high + side
            dx = dx + mm_t(
                d_store[rows, (2 - side) * C : (3 - side) * C],
                w_store[layer, tap * C : (tap + 1) * C, :],
            )
    return dx.astype(bf16), d_mixed.astype(bf16), d_logit, d_before


def backward_stage(stage, images):
    count = SIDE * images * SIDE

    def body(
        place, dy_ref, mixed_ref, pooled_ref, before_ref, gate_ref, w_store, dx_ref, d_ref, d_store, se_store
    ):
        @pl.when(place[0] == stage)
        def _():
            weights = Resident()
            dy = dy_ref[...].astype(f32)
            se_store[...] = jnp.zeros((EXTRA, C), f32)
            for layer in (1, 0):
                before = before_ref[layer]
                dx, d_mixed, d_logit, d_before = layer_backward(
                    dy, layer, weights, w_store, d_store,
                    mixed_ref[layer], before, gate_ref[layer], images,
                )
                dx_ref[layer] = dx
                d_ref[layer, :count] = d_mixed
                se_store[0:images, :] = pooled_ref[layer]
                se_store[8 : 8 + images, :] = d_logit
                se_store[16 : 16 + images, :SE] = before * jax.nn.sigmoid(before)
                se_store[16 : 16 + images, SE:] = d_before
                d_ref[layer, count:] = se_store[...].astype(bf16)
                dy = dx.astype(f32)

    return pl.pallas_call(
        body,
        out_shape=[
            jax.ShapeDtypeStruct((2, count, C), bf16),
            jax.ShapeDtypeStruct((2, count + EXTRA, C), bf16),
        ],
        in_specs=stage_specs(6, 0),
        out_specs=[pl.BlockSpec(memory_space=pltpu.VMEM)] * 2,
        scratch_shapes=shift_scratch(images) + [pltpu.VMEM((EXTRA, C), f32)],
        compiler_params=pltpu.CompilerParams(vmem_limit_bytes=14 * MIB),
        name="backward_stage",
    )


def column_rows(images, group, dp_z, dp_x):
    count = SIDE * images * SIDE
    part = ROWS // (dp_z * dp_x)

    def body(place, x_ref, out_ref, x_store, left_store):
        for piece in range(group):
            put_shifted(x_ref[piece].astype(f32), x_store, images)
            columns = slice(piece * count, (piece + 1) * count)
            for high in range(3):
                for side in range(3):
                    tap = 3 * high + side
                    rows = slice(high * images * SIDE, high * images * SIDE + count)
                    left_store[tap * C : (tap + 1) * C, columns] = x_store[
                        rows, side * C : (side + 1) * C
                    ].T
        left_store[TAPS:, :] = jnp.zeros((ROWS - TAPS, group * count), bf16)
        for z in range(dp_z):
            begin = pl.multiple_of((z * dp_x + place[3]) * part, 32)
            out_ref[z * part : (z + 1) * part, :] = left_store[pl.ds(begin, part), :]

    vmem = pl.BlockSpec(memory_space=pltpu.VMEM)
    return pl.pallas_call(
        body,
        out_shape=jax.ShapeDtypeStruct((dp_z * part, group * count), bf16),
        in_specs=[pl.BlockSpec(memory_space=pltpu.SMEM), vmem],
        out_specs=vmem,
        scratch_shapes=[
            pltpu.VMEM((count + 2 * images * SIDE, 3 * C), bf16),
            pltpu.VMEM((ROWS, group * count), bf16),
        ],
        compiler_params=pltpu.CompilerParams(vmem_limit_bytes=32 * MIB),
        name="column_rows",
    )


def weight_grad(images, dp_z, dp_x):
    count = SIDE * images * SIDE
    part = ROWS // (dp_z * dp_x)
    last = (dp_z - 1) * dp_x * part
    tall = TAPS - last
    group = 2 * dp_x

    def outer(a, b):
        return lax.dot_general(
            a.astype(bf16), b.astype(bf16), (((0,), (0,)), ((), ())), preferred_element_type=f32
        )

    def body(place, left_ref, *rest):
        pieces = rest[:5]
        out_ref, d_store, se_store, sems = rest[5:]
        x = place[3]
        copies = []
        begin = 0
        for index, ref in enumerate(pieces):
            copies.append(
                pltpu.make_async_copy(
                    ref, d_store.at[pl.ds(begin, ref.shape[0])], sems.at[index]
                )
            )
            begin += ref.shape[0]
        for copy in copies:
            copy.start()
        for copy in copies:
            copy.wait()
        d_all = d_store[:, :count, :].reshape(group * count, C)
        extra = d_store[:, count:, :].astype(f32)
        pooled = extra[:, 0:8].reshape(8 * group, C)
        d_logit = extra[:, 8:16].reshape(8 * group, C)
        hidden = extra[:, 16:24, :SE].reshape(8 * group, SE)
        d_before = extra[:, 16:24, SE:].reshape(8 * group, SE)
        even = mm(pooled.astype(bf16), selector(0))
        odd = mm(pooled.astype(bf16), selector(1))
        se_store[0:tall, :] = jnp.zeros((tall, C), f32)
        se_store[tall : tall + SE, 0:SE] = outer(even, d_before)
        se_store[tall : tall + SE, SE:] = outer(odd, d_before)
        se_store[tall + SE :, :] = outer(hidden, d_logit)
        total = mm(left_ref[...], d_all)
        cut = (dp_z - 1) * part
        out_ref[:cut, :] = total[:cut].astype(bf16)
        mine = se_store[pl.ds(pl.multiple_of(x * part, 32), part), :]
        out_ref[cut:, :] = (total[cut:] + mine).astype(bf16)

    return pl.pallas_call(
        body,
        out_shape=jax.ShapeDtypeStruct((dp_z * part, C), bf16),
        in_specs=[
            pl.BlockSpec(memory_space=pltpu.SMEM),
            pl.BlockSpec(memory_space=pltpu.VMEM),
        ]
        + [pl.BlockSpec(memory_space=pl.ANY)] * 5,
        out_specs=pl.BlockSpec(memory_space=pltpu.VMEM),
        scratch_shapes=[
            pltpu.VMEM((group, count + EXTRA, C), bf16),
            pltpu.VMEM((ROWS - last, C), f32),
            pltpu.SemaphoreType.DMA((5,)),
        ],
        compiler_params=pltpu.CompilerParams(vmem_limit_bytes=24 * MIB),
        name="weight_grad",
    )


def shift(value, axis, by):
    size = lax.axis_size(axis)
    return lax.ppermute(value, axis, [(i, (i + by) % size) for i in range(size)])


def ring(value, axis):
    steps = lax.axis_size(axis) // 2
    half = value.shape[0] // 2
    below = above = value
    found = [value]
    for step in range(steps):
        if step == steps - 1:
            below, above = below[:half], above[half:]
        below, above = shift(below, axis, 1), shift(above, axis, -1)
        found += [below, above]
    return found


def swap(value):
    return lax.ppermute(value, "core", [(0, 1), (1, 0)])


def per_device(student_in, teacher_in, out_grad, student_params, teacher_params):
    micro = student_in.shape[0]
    stages = lax.axis_size("y")
    dp_z = lax.axis_size("z")
    dp_x = lax.axis_size("x")
    y = lax.axis_index("y")
    x = lax.axis_index("x")
    z = lax.axis_index("z")
    core = lax.axis_index("core")
    first_core = core == 0
    images = micro
    count = SIDE * images * SIDE
    group = 2 * dp_x

    def own(array):
        taken = lax.dynamic_index_in_dim(array, core, 1, keepdims=False)
        return taken.transpose(1, 0, 2, 3).reshape(count, C)

    place = jnp.stack([y, core, z, x]).astype(jnp.int32)
    hits = [y == stage for stage in range(stages)]
    place, hits, first_core = lax.optimization_barrier((place, hits, first_core))

    def matrix(row):
        return row.astype(bf16).reshape(-1, C)

    def up(value, stage):
        return lax.ppermute(value, "y", [(stage, stage + 1)])

    def pick(stage, new, old):
        if old is None:
            return new
        return jax.tree.map(lambda a, b: jnp.where(hits[stage], a, b), new, old)

    def trade(pair):
        mine = jnp.where(first_core, pair[0], pair[1])
        theirs = swap(jnp.where(first_core, pair[1], pair[0]))
        return mine, theirs

    def placed(pair):
        mine, theirs = trade(pair)
        ordered = jnp.stack((jnp.where(first_core, mine, theirs), jnp.where(first_core, theirs, mine)))
        return ordered.reshape(2, SIDE, micro, SIDE, C).transpose(2, 0, 1, 3, 4)[None]

    along_x = lax.all_gather(matrix(student_params), "x", axis=0, tiled=True)
    teacher_row, along_x = lax.optimization_barrier((matrix(teacher_params), along_x))
    turned = [shift(teacher_row, "x", by) for by in range(dp_x - 1, 0, -1)] + [teacher_row]
    start = (dp_x - 1 - x) % dp_x * teacher_row.shape[0]
    pieces = ring(along_x, "z")
    teacher_x = lax.dynamic_slice_in_dim(
        jnp.concatenate(turned + turned, axis=0), start, dp_x * teacher_row.shape[0], 0
    )
    teacher_x, _ = lax.optimization_barrier((teacher_x, pieces[-2:]))
    teacher_w = lax.all_gather(teacher_x, "z", axis=0, tiled=True)
    weights = assemble(len(pieces), dp_z)(place, *pieces, *[swap(piece) for piece in pieces])

    now = own(student_in)
    kept = []
    for stage in range(stages):
        mid, out, *saved = forward_stage(stage, images, 0, 0, True)(place, now, weights)
        kept.append((now, mid, saved))
        if stage + 1 < stages:
            now = up(out, stage)

    x_in = None
    for stage in range(stages):
        x_in = pick(stage, kept[stage][:2], x_in)

    def teacher_stage(stage, now):
        return forward_stage(stage, images, 1, dp_z, False)(place, now, *teacher_pair)

    now = own(out_grad)
    back = None
    for stage in range(stages - 1, -1, -1):
        if stage == 2:
            x_in, _ = lax.optimization_barrier((x_in, new_dx))
            x_all = jnp.concatenate(ring(jnp.stack(trade(x_in)), "x"), axis=0)
            now, x_all = lax.optimization_barrier((now, x_all))
        if stage == 1:
            now, teacher_w = lax.optimization_barrier((now, teacher_w))
            teacher_pair = (teacher_w, swap(teacher_w))
        if stage == 0:
            x_late, _ = lax.optimization_barrier((x_all, new_dx))
            teacher_now, _ = lax.optimization_barrier((own(teacher_in), new_dx))
            left = column_rows(images, group, dp_z, dp_x)(place, x_late)
            teacher_out = teacher_stage(0, teacher_now)
            now, left, teacher_out = lax.optimization_barrier((now, left, teacher_out))
        new_dx, new_d = backward_stage(stage, images)(place, now, *kept[stage][2], weights)
        back = pick(stage, (new_dx, new_d), back)
        if stage > 0:
            now = lax.ppermute(new_dx[0], "y", [(stage, stage - 1)])
    dx, d_mixed = back

    d_pieces = ring(jnp.stack(trade((d_mixed[0], d_mixed[1]))), "x")
    acts = teacher_out
    teacher_out = teacher_stage(1, up(teacher_out[1], 0))
    d_pieces, teacher_out = lax.optimization_barrier((d_pieces, teacher_out))
    blocks = weight_grad(images, dp_z, dp_x)(place, left, *d_pieces)
    shard = lax.psum_scatter(blocks, "z", scatter_dimension=0, tiled=True)
    grad = shard.astype(f32).reshape(1, -1)
    teacher_new = ema_keep * teacher_params + (1.0 - ema_keep) * (student_params - step_rate * grad)

    for stage in range(1, stages):
        if stage > 1:
            teacher_out = teacher_stage(stage, up(teacher_out[1], stage - 1))
        acts = pick(stage, teacher_out, acts)

    return placed(acts), placed((dx[0], dx[1])), grad, teacher_new


def solution(mesh):
    grid = Mesh(mesh.devices.reshape(4, 2, 8, 4), ("y", "core", "z", "x"))
    seg = ("y", "core")
    dp = ("z", "x")
    image_spec = P(None, dp, None, None, None)
    return jax.shard_map(
        per_device,
        mesh=grid,
        in_specs=(image_spec, image_spec, image_spec, P(seg, dp), P(seg, dp)),
        out_specs=(
            P(seg, None, dp, None, None, None),
            P(seg, None, dp, None, None, None),
            P(seg, dp),
            P(seg, dp),
        ),
        check_vma=False,
    )
```

```python
import jax
import jax.numpy as jnp
import numpy as np
from jax import lax
from jax.experimental import pallas as pl
from jax.experimental.pallas import tpu as pltpu
from jax.sharding import Mesh, PartitionSpec as P

C = 512
SE = 256
SIDE = 8
TAPS = 9 * C
ROWS = TAPS + 2 * SE
HIGH = TAPS // 3
EXTRA = 32
MIB = 1024 * 1024

ema_keep = 0.99
step_rate = 0.001

f32 = jnp.float32
bf16 = jnp.bfloat16


def mm(a, b):
    return jnp.dot(a, b, preferred_element_type=f32)


def mm_t(a, b):
    return lax.dot_general(a, b, (((1,), (1,)), ((), ())), preferred_element_type=f32)


def selector(odd):
    channel = lax.broadcasted_iota(jnp.int32, (C, SE), 0)
    half = lax.broadcasted_iota(jnp.int32, (C, SE), 1)
    return jnp.where(channel == 2 * half + odd, 1.0, 0.0).astype(bf16)


def put_shifted(values, store, images):
    pad = images * SIDE
    count = SIDE * pad
    tiles = values.reshape(count // 8, 8, C)
    column = lax.broadcasted_iota(jnp.int32, (count // 8, 8, C), 1)
    left = jnp.where(column == 0, 0.0, pltpu.roll(tiles, 1, 1))
    right = jnp.where(column == 7, 0.0, pltpu.roll(tiles, 7, 1))
    store[0:pad, :] = jnp.zeros((pad, 3 * C), bf16)
    store[pad + count :, :] = jnp.zeros((pad, 3 * C), bf16)
    store[pad : pad + count, 0:C] = left.reshape(count, C).astype(bf16)
    store[pad : pad + count, C : 2 * C] = values.astype(bf16)
    store[pad : pad + count, 2 * C :] = right.reshape(count, C).astype(bf16)


def piece_spots(place, sizes):
    z, dp_z, rows = place[2], len(sizes) - 1, sizes[0]
    spots = [z * rows]
    for step in range(1, dp_z // 2 + 1):
        spots.append(((z + dp_z - step) % dp_z) * rows)
        high = ((z + step) % dp_z) * rows
        spots.append(high + rows // 2 if step == dp_z // 2 else high)
    return spots


class Weights:
    def __init__(self, place, own, other, store, sems, groups):
        core = place[1]
        rows = ROWS // groups
        self.store, self.sems, self.groups = store, sems, groups
        self.whole = own[0] if own[0].shape[0] == rows else own[0].at[pl.ds(0, rows), :]
        self.core = core
        self.lists = []
        for refs, slot in ((own, core), (other, 1 - core)):
            found = []
            if len(refs) == 1:
                for z in range(groups):
                    found.append(
                        pltpu.make_async_copy(
                            refs[0].at[pl.ds(z * rows, rows), :],
                            store.at[slot, pl.ds(z * rows, rows), :],
                            sems.at[slot, z],
                        )
                    )
            else:
                sizes = [ref.shape[0] for ref in refs]
                for ref, spot in zip(refs, piece_spots(place, sizes)):
                    spot = pl.multiple_of(spot, 64)
                    found.append(
                        pltpu.make_async_copy(
                            ref, store.at[slot, pl.ds(spot, ref.shape[0]), :], sems.at[slot, spot // rows]
                        )
                    )
            self.lists.append(found)

    def start(self, first):
        own, other = self.lists

        @pl.when(self.core == first)
        def _():
            for copy in own + other:
                copy.start()

        @pl.when(self.core != first)
        def _():
            for copy in other + own:
                copy.start()

    def wait(self, layer, begin, end):
        rows = ROWS // self.groups
        for z in range(begin, end):
            pltpu.make_async_copy(
                self.whole, self.store.at[layer, pl.ds(z * rows, rows), :], self.sems.at[layer, z]
            ).wait()

    def need(self, layer, high):
        rows = ROWS // self.groups
        begin = 0 if high == 0 else -(-high * HIGH // rows)
        end = self.groups if high == 2 else -(-(high + 1) * HIGH // rows)
        self.wait(layer, begin, end)


def spread(per_image, images):
    return jnp.broadcast_to(per_image.reshape(1, images, 1, C), (SIDE, images, SIDE, C)).reshape(
        SIDE * images * SIDE, C
    )


def image_sum(values, images):
    return jnp.sum(jnp.sum(values.reshape(SIDE, images, SIDE, C), axis=0), axis=1)


def assemble(pieces, groups):
    def body(place, *rest):
        own, other = rest[:pieces], rest[pieces : 2 * pieces]
        out_ref, sems = rest[2 * pieces :]
        weights = Weights(place, own, other, out_ref, sems, groups)
        weights.start(0)
        for layer in range(2):
            weights.wait(layer, 0, groups)

    return pl.pallas_call(
        body,
        out_shape=pltpu.VMEM((2, ROWS, C), bf16),
        in_specs=[pl.BlockSpec(memory_space=pltpu.SMEM)]
        + [pl.BlockSpec(memory_space=pltpu.HBM)] * (2 * pieces),
        out_specs=pl.BlockSpec(memory_space=pltpu.VMEM),
        scratch_shapes=[pltpu.SemaphoreType.DMA((2, groups))],
        compiler_params=pltpu.CompilerParams(vmem_limit_bytes=48 * MIB),
        name="assemble",
    )


class Resident:
    groups = 0

    def need(self, layer, high):
        pass

    def wait(self, layer, begin, end):
        pass


def layer_forward(x, layer, weights, w_store, x_store, images):
    count = SIDE * images * SIDE
    put_shifted(x, x_store, images)
    mixed = None
    for high in range(3):
        weights.need(layer, high)
        part = mm(
            x_store[high * images * SIDE : high * images * SIDE + count, :],
            w_store[layer, high * HIGH : (high + 1) * HIGH, :],
        )
        mixed = part if mixed is None else mixed + part
    active = mixed * jax.nn.sigmoid(mixed)
    pooled = (image_sum(active, images) * (1.0 / (SIDE * SIDE))).astype(bf16)
    reduce_w = w_store[layer, TAPS : TAPS + SE, :]
    expand_w = w_store[layer, TAPS + SE : ROWS, :]
    even = mm(pooled, selector(0)).astype(bf16)
    odd = mm(pooled, selector(1)).astype(bf16)
    before = mm(even, reduce_w[:, :SE]) + mm(odd, reduce_w[:, SE:])
    hidden = (before * jax.nn.sigmoid(before)).astype(bf16)
    gate = jax.nn.sigmoid(mm(hidden, expand_w))
    out = x + active * spread(gate, images)
    return out.astype(bf16), mixed, pooled, before, gate


def stage_specs(vmem_inputs, pieces):
    return (
        [pl.BlockSpec(memory_space=pltpu.SMEM)]
        + [pl.BlockSpec(memory_space=pltpu.VMEM)] * vmem_inputs
        + [pl.BlockSpec(memory_space=pltpu.HBM)] * (2 * pieces)
    )


def shift_scratch(images):
    return [pltpu.VMEM(((SIDE + 2) * images * SIDE, 3 * C), bf16)]


def store_scratch(groups):
    return [pltpu.VMEM((2, ROWS, C), bf16), pltpu.SemaphoreType.DMA((2, groups))]


def forward_stage(stage, images, pieces, groups, keep):
    count = SIDE * images * SIDE

    def body(place, x_ref, *rest):
        if keep:
            w_store, mid_ref, out_ref, *saved = rest[:-1]
            x_store = rest[-1]
        else:
            own, other = rest[:pieces], rest[pieces : 2 * pieces]
            mid_ref, out_ref, *saved = rest[2 * pieces : -3]
            x_store, w_store, sems = rest[-3:]

        @pl.when(place[0] == stage)
        def _():
            if keep:
                weights = Resident()
            else:
                weights = Weights(place, own, other, w_store, sems, groups)
                weights.start(0)
            x = x_ref[...].astype(f32)
            for layer in range(2):
                out, mixed, pooled, before, gate = layer_forward(
                    x, layer, weights, w_store, x_store, images
                )
                (mid_ref, out_ref)[layer][...] = out
                if keep:
                    mixed_ref, pooled_ref, before_ref, gate_ref = saved
                    mixed_ref[layer] = mixed
                    pooled_ref[layer] = pooled.astype(f32)
                    before_ref[layer] = before
                    gate_ref[layer] = gate
                x = out.astype(f32)

    shapes = [jax.ShapeDtypeStruct((count, C), bf16)] * 2
    if keep:
        shapes += [
            jax.ShapeDtypeStruct((2, count, C), f32),
            jax.ShapeDtypeStruct((2, images, C), f32),
            jax.ShapeDtypeStruct((2, images, SE), f32),
            jax.ShapeDtypeStruct((2, images, C), f32),
        ]
    return pl.pallas_call(
        body,
        out_shape=shapes,
        in_specs=stage_specs(2, 0) if keep else stage_specs(1, pieces),
        out_specs=[pl.BlockSpec(memory_space=pltpu.VMEM)] * len(shapes),
        scratch_shapes=shift_scratch(images) + ([] if keep else store_scratch(groups)),
        compiler_params=pltpu.CompilerParams(vmem_limit_bytes=(14 if keep else 24) * MIB),
        name="forward_stage",
    )


def layer_backward(dy, layer, weights, w_store, d_store, mixed, before, gate, images):
    count = SIDE * images * SIDE
    sig = jax.nn.sigmoid(mixed)
    active = mixed * sig
    d_gate = image_sum(dy * active, images)
    d_logit = d_gate * gate * (1.0 - gate)
    weights.wait(layer, 0, weights.groups)
    reduce_w = w_store[layer, TAPS : TAPS + SE, :]
    expand_w = w_store[layer, TAPS + SE : ROWS, :]
    d_hidden = mm_t(d_logit.astype(bf16), expand_w).astype(bf16).astype(f32)
    soft = jax.nn.sigmoid(before)
    d_before = d_hidden * (soft + before * soft * (1.0 - soft))
    low = d_before.astype(bf16)
    d_even = mm_t(low, reduce_w[:, :SE]).astype(bf16)
    d_odd = mm_t(low, reduce_w[:, SE:]).astype(bf16)
    d_pooled = mm_t(d_even, selector(0)) + mm_t(d_odd, selector(1))
    d_active = dy * spread(gate, images) + spread(d_pooled * (1.0 / (SIDE * SIDE)), images)
    d_mixed = d_active * (sig + active * (1.0 - sig))
    put_shifted(d_mixed, d_store, images)
    dx = dy
    for high in range(3):
        rows = slice((2 - high) * images * SIDE, (2 - high) * images * SIDE + count)
        for side in range(3):
            tap = 3 * high + side
            dx = dx + mm_t(
                d_store[rows, (2 - side) * C : (3 - side) * C],
                w_store[layer, tap * C : (tap + 1) * C, :],
            )
    return dx.astype(bf16), d_mixed.astype(bf16), d_logit, d_before


def backward_stage(stage, images):
    count = SIDE * images * SIDE

    def body(
        place, dy_ref, mixed_ref, pooled_ref, before_ref, gate_ref, w_store, dx_ref, d_ref, d_store, se_store
    ):
        @pl.when(place[0] == stage)
        def _():
            weights = Resident()
            dy = dy_ref[...].astype(f32)
            se_store[...] = jnp.zeros((EXTRA, C), f32)
            for layer in (1, 0):
                before = before_ref[layer]
                dx, d_mixed, d_logit, d_before = layer_backward(
                    dy, layer, weights, w_store, d_store,
                    mixed_ref[layer], before, gate_ref[layer], images,
                )
                dx_ref[layer] = dx
                d_ref[layer, :count] = d_mixed
                se_store[0:images, :] = pooled_ref[layer]
                se_store[8 : 8 + images, :] = d_logit
                se_store[16 : 16 + images, :SE] = before * jax.nn.sigmoid(before)
                se_store[16 : 16 + images, SE:] = d_before
                d_ref[layer, count:] = se_store[...].astype(bf16)
                dy = dx.astype(f32)

    return pl.pallas_call(
        body,
        out_shape=[
            jax.ShapeDtypeStruct((2, count, C), bf16),
            jax.ShapeDtypeStruct((2, count + EXTRA, C), bf16),
        ],
        in_specs=stage_specs(6, 0),
        out_specs=[pl.BlockSpec(memory_space=pltpu.VMEM)] * 2,
        scratch_shapes=shift_scratch(images) + [pltpu.VMEM((EXTRA, C), f32)],
        compiler_params=pltpu.CompilerParams(vmem_limit_bytes=14 * MIB),
        name="backward_stage",
    )


def column_rows(images, group, dp_z, dp_x):
    count = SIDE * images * SIDE
    part = ROWS // (dp_z * dp_x)

    def body(place, x_ref, out_ref, x_store, left_store):
        for piece in range(group):
            put_shifted(x_ref[piece].astype(f32), x_store, images)
            columns = slice(piece * count, (piece + 1) * count)
            for high in range(3):
                for side in range(3):
                    tap = 3 * high + side
                    rows = slice(high * images * SIDE, high * images * SIDE + count)
                    left_store[tap * C : (tap + 1) * C, columns] = x_store[
                        rows, side * C : (side + 1) * C
                    ].T
        left_store[TAPS:, :] = jnp.zeros((ROWS - TAPS, group * count), bf16)
        for z in range(dp_z):
            begin = pl.multiple_of((z * dp_x + place[3]) * part, 32)
            out_ref[z * part : (z + 1) * part, :] = left_store[pl.ds(begin, part), :]

    vmem = pl.BlockSpec(memory_space=pltpu.VMEM)
    return pl.pallas_call(
        body,
        out_shape=jax.ShapeDtypeStruct((dp_z * part, group * count), bf16),
        in_specs=[pl.BlockSpec(memory_space=pltpu.SMEM), vmem],
        out_specs=vmem,
        scratch_shapes=[
            pltpu.VMEM((count + 2 * images * SIDE, 3 * C), bf16),
            pltpu.VMEM((ROWS, group * count), bf16),
        ],
        compiler_params=pltpu.CompilerParams(vmem_limit_bytes=32 * MIB),
        name="column_rows",
    )


def weight_grad(images, dp_z, dp_x):
    count = SIDE * images * SIDE
    part = ROWS // (dp_z * dp_x)
    last = (dp_z - 1) * dp_x * part
    tall = TAPS - last
    group = 2 * dp_x

    def outer(a, b):
        return lax.dot_general(
            a.astype(bf16), b.astype(bf16), (((0,), (0,)), ((), ())), preferred_element_type=f32
        )

    def body(place, left_ref, *rest):
        pieces = rest[:5]
        out_ref, d_store, se_store, sems = rest[5:]
        x = place[3]
        copies = []
        begin = 0
        for index, ref in enumerate(pieces):
            copies.append(
                pltpu.make_async_copy(
                    ref, d_store.at[pl.ds(begin, ref.shape[0])], sems.at[index]
                )
            )
            begin += ref.shape[0]
        for copy in copies:
            copy.start()
        for copy in copies:
            copy.wait()
        d_all = d_store[:, :count, :].reshape(group * count, C)
        extra = d_store[:, count:, :].astype(f32)
        pooled = extra[:, 0:8].reshape(8 * group, C)
        d_logit = extra[:, 8:16].reshape(8 * group, C)
        hidden = extra[:, 16:24, :SE].reshape(8 * group, SE)
        d_before = extra[:, 16:24, SE:].reshape(8 * group, SE)
        even = mm(pooled.astype(bf16), selector(0))
        odd = mm(pooled.astype(bf16), selector(1))
        se_store[0:tall, :] = jnp.zeros((tall, C), f32)
        se_store[tall : tall + SE, 0:SE] = outer(even, d_before)
        se_store[tall : tall + SE, SE:] = outer(odd, d_before)
        se_store[tall + SE :, :] = outer(hidden, d_logit)
        total = mm(left_ref[...], d_all)
        cut = (dp_z - 1) * part
        out_ref[:cut, :] = total[:cut].astype(bf16)
        mine = se_store[pl.ds(pl.multiple_of(x * part, 32), part), :]
        out_ref[cut:, :] = (total[cut:] + mine).astype(bf16)

    return pl.pallas_call(
        body,
        out_shape=jax.ShapeDtypeStruct((dp_z * part, C), bf16),
        in_specs=[
            pl.BlockSpec(memory_space=pltpu.SMEM),
            pl.BlockSpec(memory_space=pltpu.VMEM),
        ]
        + [pl.BlockSpec(memory_space=pl.ANY)] * 5,
        out_specs=pl.BlockSpec(memory_space=pltpu.VMEM),
        scratch_shapes=[
            pltpu.VMEM((group, count + EXTRA, C), bf16),
            pltpu.VMEM((ROWS - last, C), f32),
            pltpu.SemaphoreType.DMA((5,)),
        ],
        compiler_params=pltpu.CompilerParams(vmem_limit_bytes=24 * MIB),
        name="weight_grad",
    )


def shift(value, axis, by):
    size = lax.axis_size(axis)
    return lax.ppermute(value, axis, [(i, (i + by) % size) for i in range(size)])


def ring(value, axis, before_last=None):
    steps = lax.axis_size(axis) // 2
    half = value.shape[0] // 2
    below = above = value
    found = [value]
    for step in range(steps):
        if step == steps - 1:
            if before_last is not None:
                below, above = before_last(below, above)
            below, above = below[:half], above[half:]
        below, above = shift(below, axis, 1), shift(above, axis, -1)
        found += [below, above]
    return found


def swap(value):
    return lax.ppermute(value, "core", [(0, 1), (1, 0)])


def per_device(student_in, teacher_in, out_grad, student_params, teacher_params):
    micro = student_in.shape[0]
    stages = lax.axis_size("y")
    dp_z = lax.axis_size("z")
    dp_x = lax.axis_size("x")
    y = lax.axis_index("y")
    x = lax.axis_index("x")
    z = lax.axis_index("z")
    core = lax.axis_index("core")
    first_core = core == 0
    images = micro
    count = SIDE * images * SIDE
    group = 2 * dp_x

    def own(array):
        taken = lax.dynamic_index_in_dim(array, core, 1, keepdims=False)
        return taken.transpose(1, 0, 2, 3).reshape(count, C)

    place = jnp.stack([y, core, z, x]).astype(jnp.int32)
    hits = [y == stage for stage in range(stages)]
    place, hits, first_core = lax.optimization_barrier((place, hits, first_core))

    def matrix(row):
        return row.astype(bf16).reshape(-1, C)

    def up(value, stage):
        return lax.ppermute(value, "y", [(stage, stage + 1)])

    def pick(stage, new, old):
        if old is None:
            return new
        return jax.tree.map(lambda a, b: jnp.where(hits[stage], a, b), new, old)

    def trade(pair):
        mine = jnp.where(first_core, pair[0], pair[1])
        theirs = swap(jnp.where(first_core, pair[1], pair[0]))
        return mine, theirs

    def placed(pair):
        mine, theirs = trade(pair)
        ordered = jnp.stack((jnp.where(first_core, mine, theirs), jnp.where(first_core, theirs, mine)))
        return ordered.reshape(2, SIDE, micro, SIDE, C).transpose(2, 0, 1, 3, 4)[None]

    along_x = lax.all_gather(matrix(student_params), "x", axis=0, tiled=True)
    teacher_row, along_x = lax.optimization_barrier((matrix(teacher_params), along_x))
    turned = [shift(teacher_row, "x", by) for by in range(dp_x - 1, 0, -1)] + [teacher_row]
    start = (dp_x - 1 - x) % dp_x * teacher_row.shape[0]
    pieces = ring(along_x, "z")
    teacher_x = lax.dynamic_slice_in_dim(
        jnp.concatenate(turned + turned, axis=0), start, dp_x * teacher_row.shape[0], 0
    )
    teacher_x, _ = lax.optimization_barrier((teacher_x, pieces[-2:]))
    teacher_w = lax.all_gather(teacher_x, "z", axis=0, tiled=True)
    weights = assemble(len(pieces), dp_z)(place, *pieces, *[swap(piece) for piece in pieces])

    now = own(student_in)
    kept = []
    for stage in range(stages):
        mid, out, *saved = forward_stage(stage, images, 0, 0, True)(place, now, weights)
        kept.append((now, mid, saved))
        if stage + 1 < stages:
            now = up(out, stage)

    x_in = None
    for stage in range(stages):
        x_in = pick(stage, kept[stage][:2], x_in)

    def teacher_stage(stage, now):
        return forward_stage(stage, images, 1, dp_z, False)(place, now, *teacher_pair)

    now = own(out_grad)
    back = None
    for stage in range(stages - 1, -1, -1):
        if stage == 2:
            x_in, _ = lax.optimization_barrier((x_in, new_dx))
            x_all = jnp.concatenate(ring(jnp.stack(trade(x_in)), "x"), axis=0)
            now, x_all = lax.optimization_barrier((now, x_all))
        if stage == 1:
            teacher_pair = (teacher_w, swap(teacher_w))
        if stage == 0:
            x_late, _ = lax.optimization_barrier((x_all, new_dx))
            teacher_now, _ = lax.optimization_barrier((own(teacher_in), new_dx))
            left = column_rows(images, group, dp_z, dp_x)(place, x_late)
            teacher_out = teacher_stage(0, teacher_now)
            now, left, teacher_out = lax.optimization_barrier((now, left, teacher_out))
        new_dx, new_d = backward_stage(stage, images)(place, now, *kept[stage][2], weights)
        back = pick(stage, (new_dx, new_d), back)
        if stage > 0:
            sent = new_dx[0]
            if stage == 2:
                sent, teacher_w = lax.optimization_barrier((sent, teacher_w))
            now = lax.ppermute(sent, "y", [(stage, stage - 1)])
    dx, d_mixed = back

    acts = teacher_out
    d_mixed, teacher_now = lax.optimization_barrier((d_mixed, up(teacher_out[1], 0)))
    teacher_out = teacher_stage(1, teacher_now)

    def after_teacher(below, above):
        nonlocal teacher_out
        below, above, teacher_out = lax.optimization_barrier((below, above, teacher_out))
        return below, above

    d_pieces = ring(jnp.stack(trade((d_mixed[0], d_mixed[1]))), "x", after_teacher)
    blocks = weight_grad(images, dp_z, dp_x)(place, left, *d_pieces)
    shard = lax.psum_scatter(blocks, "z", scatter_dimension=0, tiled=True)
    grad = shard.astype(f32).reshape(1, -1)
    teacher_new = ema_keep * teacher_params + (1.0 - ema_keep) * (student_params - step_rate * grad)

    for stage in range(1, stages):
        if stage > 1:
            teacher_out = teacher_stage(stage, up(teacher_out[1], stage - 1))
        acts = pick(stage, teacher_out, acts)

    return placed(acts), placed((dx[0], dx[1])), grad, teacher_new


def solution(mesh):
    grid = Mesh(mesh.devices.reshape(4, 2, 8, 4), ("y", "core", "z", "x"))
    seg = ("y", "core")
    dp = ("z", "x")
    image_spec = P(None, dp, None, None, None)
    return jax.shard_map(
        per_device,
        mesh=grid,
        in_specs=(image_spec, image_spec, image_spec, P(seg, dp), P(seg, dp)),
        out_specs=(
            P(seg, None, dp, None, None, None),
            P(seg, None, dp, None, None, None),
            P(seg, dp),
            P(seg, dp),
        ),
        check_vma=False,
    )
```

```python
import jax
import jax.numpy as jnp
import numpy as np
from jax import lax
from jax.experimental import pallas as pl
from jax.experimental.pallas import tpu as pltpu
from jax.sharding import Mesh, PartitionSpec as P

C = 512
SE = 256
SIDE = 8
TAPS = 9 * C
ROWS = TAPS + 2 * SE
HIGH = TAPS // 3
EXTRA = 32
MIB = 1024 * 1024

ema_keep = 0.99
step_rate = 0.001

f32 = jnp.float32
bf16 = jnp.bfloat16


def mm(a, b):
    return jnp.dot(a, b, preferred_element_type=f32)


def mm_t(a, b):
    return lax.dot_general(a, b, (((1,), (1,)), ((), ())), preferred_element_type=f32)


def selector(odd):
    channel = lax.broadcasted_iota(jnp.int32, (C, SE), 0)
    half = lax.broadcasted_iota(jnp.int32, (C, SE), 1)
    return jnp.where(channel == 2 * half + odd, 1.0, 0.0).astype(bf16)


def put_shifted(values, store, images):
    pad = images * SIDE
    count = SIDE * pad
    tiles = values.reshape(count // 8, 8, C)
    column = lax.broadcasted_iota(jnp.int32, (count // 8, 8, C), 1)
    left = jnp.where(column == 0, 0.0, pltpu.roll(tiles, 1, 1))
    right = jnp.where(column == 7, 0.0, pltpu.roll(tiles, 7, 1))
    store[0:pad, :] = jnp.zeros((pad, 3 * C), bf16)
    store[pad + count :, :] = jnp.zeros((pad, 3 * C), bf16)
    store[pad : pad + count, 0:C] = left.reshape(count, C).astype(bf16)
    store[pad : pad + count, C : 2 * C] = values.astype(bf16)
    store[pad : pad + count, 2 * C :] = right.reshape(count, C).astype(bf16)


def piece_spots(place, sizes):
    z, dp_z, rows = place[2], len(sizes) - 1, sizes[0]
    spots = [z * rows]
    for step in range(1, dp_z // 2 + 1):
        spots.append(((z + dp_z - step) % dp_z) * rows)
        high = ((z + step) % dp_z) * rows
        spots.append(high + rows // 2 if step == dp_z // 2 else high)
    return spots


class Weights:
    def __init__(self, place, own, other, store, sems, groups):
        core = place[1]
        rows = ROWS // groups
        self.store, self.sems, self.groups = store, sems, groups
        self.whole = own[0] if own[0].shape[0] == rows else own[0].at[pl.ds(0, rows), :]
        self.core = core
        self.lists = []
        for refs, slot in ((own, core), (other, 1 - core)):
            found = []
            if len(refs) == 1:
                for z in range(groups):
                    found.append(
                        pltpu.make_async_copy(
                            refs[0].at[pl.ds(z * rows, rows), :],
                            store.at[slot, pl.ds(z * rows, rows), :],
                            sems.at[slot, z],
                        )
                    )
            else:
                sizes = [ref.shape[0] for ref in refs]
                for ref, spot in zip(refs, piece_spots(place, sizes)):
                    spot = pl.multiple_of(spot, 64)
                    found.append(
                        pltpu.make_async_copy(
                            ref, store.at[slot, pl.ds(spot, ref.shape[0]), :], sems.at[slot, spot // rows]
                        )
                    )
            self.lists.append(found)

    def start(self, first):
        own, other = self.lists

        @pl.when(self.core == first)
        def _():
            for copy in own + other:
                copy.start()

        @pl.when(self.core != first)
        def _():
            for copy in other + own:
                copy.start()

    def wait(self, layer, begin, end):
        rows = ROWS // self.groups
        for z in range(begin, end):
            pltpu.make_async_copy(
                self.whole, self.store.at[layer, pl.ds(z * rows, rows), :], self.sems.at[layer, z]
            ).wait()

    def need(self, layer, high):
        rows = ROWS // self.groups
        begin = 0 if high == 0 else -(-high * HIGH // rows)
        end = self.groups if high == 2 else -(-(high + 1) * HIGH // rows)
        self.wait(layer, begin, end)


def spread(per_image, images):
    return jnp.broadcast_to(per_image.reshape(1, images, 1, C), (SIDE, images, SIDE, C)).reshape(
        SIDE * images * SIDE, C
    )


def image_sum(values, images):
    return jnp.sum(jnp.sum(values.reshape(SIDE, images, SIDE, C), axis=0), axis=1)


def assemble(pieces, groups):
    def body(place, *rest):
        own, other = rest[:pieces], rest[pieces : 2 * pieces]
        out_ref, sems = rest[2 * pieces :]
        weights = Weights(place, own, other, out_ref, sems, groups)
        weights.start(0)
        for layer in range(2):
            weights.wait(layer, 0, groups)

    return pl.pallas_call(
        body,
        out_shape=pltpu.VMEM((2, ROWS, C), bf16),
        in_specs=[pl.BlockSpec(memory_space=pltpu.SMEM)]
        + [pl.BlockSpec(memory_space=pltpu.HBM)] * (2 * pieces),
        out_specs=pl.BlockSpec(memory_space=pltpu.VMEM),
        scratch_shapes=[pltpu.SemaphoreType.DMA((2, groups))],
        compiler_params=pltpu.CompilerParams(vmem_limit_bytes=48 * MIB),
        name="assemble",
    )


class Resident:
    groups = 0

    def need(self, layer, high):
        pass

    def wait(self, layer, begin, end):
        pass


def layer_forward(x, layer, weights, w_store, x_store, images):
    count = SIDE * images * SIDE
    put_shifted(x, x_store, images)
    mixed = None
    for high in range(3):
        weights.need(layer, high)
        part = mm(
            x_store[high * images * SIDE : high * images * SIDE + count, :],
            w_store[layer, high * HIGH : (high + 1) * HIGH, :],
        )
        mixed = part if mixed is None else mixed + part
    active = mixed * jax.nn.sigmoid(mixed)
    pooled = (image_sum(active, images) * (1.0 / (SIDE * SIDE))).astype(bf16)
    reduce_w = w_store[layer, TAPS : TAPS + SE, :]
    expand_w = w_store[layer, TAPS + SE : ROWS, :]
    even = mm(pooled, selector(0)).astype(bf16)
    odd = mm(pooled, selector(1)).astype(bf16)
    before = mm(even, reduce_w[:, :SE]) + mm(odd, reduce_w[:, SE:])
    hidden = (before * jax.nn.sigmoid(before)).astype(bf16)
    gate = jax.nn.sigmoid(mm(hidden, expand_w))
    out = x + active * spread(gate, images)
    return out.astype(bf16), mixed, pooled, before, gate


def stage_specs(vmem_inputs, pieces):
    return (
        [pl.BlockSpec(memory_space=pltpu.SMEM)]
        + [pl.BlockSpec(memory_space=pltpu.VMEM)] * vmem_inputs
        + [pl.BlockSpec(memory_space=pltpu.HBM)] * (2 * pieces)
    )


def shift_scratch(images):
    return [pltpu.VMEM(((SIDE + 2) * images * SIDE, 3 * C), bf16)]


def store_scratch(groups):
    return [pltpu.VMEM((2, ROWS, C), bf16), pltpu.SemaphoreType.DMA((2, groups))]


def forward_stage(stage, images, pieces, groups, keep):
    count = SIDE * images * SIDE

    def body(place, x_ref, *rest):
        if keep:
            w_store, mid_ref, out_ref, *saved = rest[:-1]
            x_store = rest[-1]
        else:
            own, other = rest[:pieces], rest[pieces : 2 * pieces]
            mid_ref, out_ref, *saved = rest[2 * pieces : -3]
            x_store, w_store, sems = rest[-3:]

        @pl.when(place[0] == stage)
        def _():
            if keep:
                weights = Resident()
            else:
                weights = Weights(place, own, other, w_store, sems, groups)
                weights.start(0)
            x = x_ref[...].astype(f32)
            for layer in range(2):
                out, mixed, pooled, before, gate = layer_forward(
                    x, layer, weights, w_store, x_store, images
                )
                (mid_ref, out_ref)[layer][...] = out
                if keep:
                    mixed_ref, pooled_ref, before_ref, gate_ref = saved
                    mixed_ref[layer] = mixed
                    pooled_ref[layer] = pooled.astype(f32)
                    before_ref[layer] = before
                    gate_ref[layer] = gate
                x = out.astype(f32)

    shapes = [jax.ShapeDtypeStruct((count, C), bf16)] * 2
    if keep:
        shapes += [
            jax.ShapeDtypeStruct((2, count, C), f32),
            jax.ShapeDtypeStruct((2, images, C), f32),
            jax.ShapeDtypeStruct((2, images, SE), f32),
            jax.ShapeDtypeStruct((2, images, C), f32),
        ]
    return pl.pallas_call(
        body,
        out_shape=shapes,
        in_specs=stage_specs(2, 0) if keep else stage_specs(1, pieces),
        out_specs=[pl.BlockSpec(memory_space=pltpu.VMEM)] * len(shapes),
        scratch_shapes=shift_scratch(images) + ([] if keep else store_scratch(groups)),
        compiler_params=pltpu.CompilerParams(vmem_limit_bytes=(14 if keep else 24) * MIB),
        name="forward_stage",
    )


def layer_backward(dy, layer, weights, w_store, d_store, mixed, before, gate, images):
    count = SIDE * images * SIDE
    sig = jax.nn.sigmoid(mixed)
    active = mixed * sig
    d_gate = image_sum(dy * active, images)
    d_logit = d_gate * gate * (1.0 - gate)
    weights.wait(layer, 0, weights.groups)
    reduce_w = w_store[layer, TAPS : TAPS + SE, :]
    expand_w = w_store[layer, TAPS + SE : ROWS, :]
    d_hidden = mm_t(d_logit.astype(bf16), expand_w).astype(bf16).astype(f32)
    soft = jax.nn.sigmoid(before)
    d_before = d_hidden * (soft + before * soft * (1.0 - soft))
    low = d_before.astype(bf16)
    d_even = mm_t(low, reduce_w[:, :SE]).astype(bf16)
    d_odd = mm_t(low, reduce_w[:, SE:]).astype(bf16)
    d_pooled = mm_t(d_even, selector(0)) + mm_t(d_odd, selector(1))
    d_active = dy * spread(gate, images) + spread(d_pooled * (1.0 / (SIDE * SIDE)), images)
    d_mixed = d_active * (sig + active * (1.0 - sig))
    put_shifted(d_mixed, d_store, images)
    dx = dy
    for high in range(3):
        rows = slice((2 - high) * images * SIDE, (2 - high) * images * SIDE + count)
        for side in range(3):
            tap = 3 * high + side
            dx = dx + mm_t(
                d_store[rows, (2 - side) * C : (3 - side) * C],
                w_store[layer, tap * C : (tap + 1) * C, :],
            )
    return dx.astype(bf16), d_mixed.astype(bf16), d_logit, d_before


def backward_stage(stage, images):
    count = SIDE * images * SIDE

    def body(
        place, dy_ref, mixed_ref, pooled_ref, before_ref, gate_ref, w_store, dx_ref, d_ref, d_store, se_store
    ):
        @pl.when(place[0] == stage)
        def _():
            weights = Resident()
            dy = dy_ref[...].astype(f32)
            se_store[...] = jnp.zeros((EXTRA, C), f32)
            for layer in (1, 0):
                before = before_ref[layer]
                dx, d_mixed, d_logit, d_before = layer_backward(
                    dy, layer, weights, w_store, d_store,
                    mixed_ref[layer], before, gate_ref[layer], images,
                )
                dx_ref[layer] = dx
                d_ref[layer, :count] = d_mixed
                se_store[0:images, :] = pooled_ref[layer]
                se_store[8 : 8 + images, :] = d_logit
                se_store[16 : 16 + images, :SE] = before * jax.nn.sigmoid(before)
                se_store[16 : 16 + images, SE:] = d_before
                d_ref[layer, count:] = se_store[...].astype(bf16)
                dy = dx.astype(f32)

    return pl.pallas_call(
        body,
        out_shape=[
            jax.ShapeDtypeStruct((2, count, C), bf16),
            jax.ShapeDtypeStruct((2, count + EXTRA, C), bf16),
        ],
        in_specs=stage_specs(6, 0),
        out_specs=[pl.BlockSpec(memory_space=pltpu.VMEM)] * 2,
        scratch_shapes=shift_scratch(images) + [pltpu.VMEM((EXTRA, C), f32)],
        compiler_params=pltpu.CompilerParams(vmem_limit_bytes=14 * MIB),
        name="backward_stage",
    )


def column_rows(images, group, dp_z, dp_x):
    count = SIDE * images * SIDE
    part = ROWS // (dp_z * dp_x)

    def body(place, x_ref, out_ref, x_store, left_store):
        for piece in range(group):
            put_shifted(x_ref[piece].astype(f32), x_store, images)
            columns = slice(piece * count, (piece + 1) * count)
            for high in range(3):
                for side in range(3):
                    tap = 3 * high + side
                    rows = slice(high * images * SIDE, high * images * SIDE + count)
                    left_store[tap * C : (tap + 1) * C, columns] = x_store[
                        rows, side * C : (side + 1) * C
                    ].T
        left_store[TAPS:, :] = jnp.zeros((ROWS - TAPS, group * count), bf16)
        for z in range(dp_z):
            begin = pl.multiple_of((z * dp_x + place[3]) * part, 32)
            out_ref[z * part : (z + 1) * part, :] = left_store[pl.ds(begin, part), :]

    vmem = pl.BlockSpec(memory_space=pltpu.VMEM)
    return pl.pallas_call(
        body,
        out_shape=jax.ShapeDtypeStruct((dp_z * part, group * count), bf16),
        in_specs=[pl.BlockSpec(memory_space=pltpu.SMEM), vmem],
        out_specs=vmem,
        scratch_shapes=[
            pltpu.VMEM((count + 2 * images * SIDE, 3 * C), bf16),
            pltpu.VMEM((ROWS, group * count), bf16),
        ],
        compiler_params=pltpu.CompilerParams(vmem_limit_bytes=32 * MIB),
        name="column_rows",
    )


def weight_grad(images, dp_z, dp_x):
    count = SIDE * images * SIDE
    part = ROWS // (dp_z * dp_x)
    last = (dp_z - 1) * dp_x * part
    tall = TAPS - last
    group = 2 * dp_x

    def outer(a, b):
        return lax.dot_general(
            a.astype(bf16), b.astype(bf16), (((0,), (0,)), ((), ())), preferred_element_type=f32
        )

    def body(place, left_ref, *rest):
        pieces = rest[:5]
        out_ref, d_store, se_store, sems = rest[5:]
        x = place[3]
        copies = []
        begin = 0
        for index, ref in enumerate(pieces):
            copies.append(
                pltpu.make_async_copy(
                    ref, d_store.at[pl.ds(begin, ref.shape[0])], sems.at[index]
                )
            )
            begin += ref.shape[0]
        for copy in copies:
            copy.start()
        for copy in copies:
            copy.wait()
        d_all = d_store[:, :count, :].reshape(group * count, C)
        extra = d_store[:, count:, :].astype(f32)
        pooled = extra[:, 0:8].reshape(8 * group, C)
        d_logit = extra[:, 8:16].reshape(8 * group, C)
        hidden = extra[:, 16:24, :SE].reshape(8 * group, SE)
        d_before = extra[:, 16:24, SE:].reshape(8 * group, SE)
        even = mm(pooled.astype(bf16), selector(0))
        odd = mm(pooled.astype(bf16), selector(1))
        se_store[0:tall, :] = jnp.zeros((tall, C), f32)
        se_store[tall : tall + SE, 0:SE] = outer(even, d_before)
        se_store[tall : tall + SE, SE:] = outer(odd, d_before)
        se_store[tall + SE :, :] = outer(hidden, d_logit)
        total = mm(left_ref[...], d_all)
        cut = (dp_z - 1) * part
        out_ref[:cut, :] = total[:cut].astype(bf16)
        mine = se_store[pl.ds(pl.multiple_of(x * part, 32), part), :]
        out_ref[cut:, :] = (total[cut:] + mine).astype(bf16)

    return pl.pallas_call(
        body,
        out_shape=jax.ShapeDtypeStruct((dp_z * part, C), bf16),
        in_specs=[
            pl.BlockSpec(memory_space=pltpu.SMEM),
            pl.BlockSpec(memory_space=pltpu.VMEM),
        ]
        + [pl.BlockSpec(memory_space=pl.ANY)] * 5,
        out_specs=pl.BlockSpec(memory_space=pltpu.VMEM),
        scratch_shapes=[
            pltpu.VMEM((group, count + EXTRA, C), bf16),
            pltpu.VMEM((ROWS - last, C), f32),
            pltpu.SemaphoreType.DMA((5,)),
        ],
        compiler_params=pltpu.CompilerParams(vmem_limit_bytes=24 * MIB),
        name="weight_grad",
    )


def shift(value, axis, by):
    size = lax.axis_size(axis)
    return lax.ppermute(value, axis, [(i, (i + by) % size) for i in range(size)])


def ring(value, axis, before_last=None):
    steps = lax.axis_size(axis) // 2
    half = value.shape[0] // 2
    below = above = value
    found = [value]
    for step in range(steps):
        if step == steps - 1:
            if before_last is not None:
                below, above = before_last(below, above)
            below, above = below[:half], above[half:]
        below, above = shift(below, axis, 1), shift(above, axis, -1)
        found += [below, above]
    return found


def swap(value):
    return lax.ppermute(value, "core", [(0, 1), (1, 0)])


def per_device(student_in, teacher_in, out_grad, student_params, teacher_params):
    micro = student_in.shape[0]
    stages = lax.axis_size("y")
    dp_z = lax.axis_size("z")
    dp_x = lax.axis_size("x")
    y = lax.axis_index("y")
    x = lax.axis_index("x")
    z = lax.axis_index("z")
    core = lax.axis_index("core")
    first_core = core == 0
    images = micro
    count = SIDE * images * SIDE
    group = 2 * dp_x

    def own(array):
        taken = lax.dynamic_index_in_dim(array, core, 1, keepdims=False)
        return taken.transpose(1, 0, 2, 3).reshape(count, C)

    place = jnp.stack([y, core, z, x]).astype(jnp.int32)
    hits = [y == stage for stage in range(stages)]
    place, hits, first_core = lax.optimization_barrier((place, hits, first_core))

    def matrix(row):
        return row.astype(bf16).reshape(-1, C)

    def up(value, stage):
        return lax.ppermute(value, "y", [(stage, stage + 1)])

    def pick(stage, new, old):
        if old is None:
            return new
        return jax.tree.map(lambda a, b: jnp.where(hits[stage], a, b), new, old)

    def trade(pair):
        mine = jnp.where(first_core, pair[0], pair[1])
        theirs = swap(jnp.where(first_core, pair[1], pair[0]))
        return mine, theirs

    def placed(pair):
        mine, theirs = trade(pair)
        ordered = jnp.stack((jnp.where(first_core, mine, theirs), jnp.where(first_core, theirs, mine)))
        return ordered.reshape(2, SIDE, micro, SIDE, C).transpose(2, 0, 1, 3, 4)[None]

    along_x = lax.all_gather(matrix(student_params), "x", axis=0, tiled=True)
    teacher_row, along_x = lax.optimization_barrier((matrix(teacher_params), along_x))
    turned = [shift(teacher_row, "x", by) for by in range(dp_x - 1, 0, -1)] + [teacher_row]
    start = (dp_x - 1 - x) % dp_x * teacher_row.shape[0]
    pieces = ring(along_x, "z")
    teacher_x = lax.dynamic_slice_in_dim(
        jnp.concatenate(turned + turned, axis=0), start, dp_x * teacher_row.shape[0], 0
    )
    teacher_x, _ = lax.optimization_barrier((teacher_x, pieces[-2:]))
    teacher_w = lax.all_gather(teacher_x, "z", axis=0, tiled=True)
    weights = assemble(len(pieces), dp_z)(place, *pieces, *[swap(piece) for piece in pieces])

    now = own(student_in)
    kept = []
    for stage in range(stages):
        mid, out, *saved = forward_stage(stage, images, 0, 0, True)(place, now, weights)
        kept.append((now, mid, saved))
        if stage + 1 < stages:
            now = up(out, stage)

    x_in = None
    for stage in range(stages):
        x_in = pick(stage, kept[stage][:2], x_in)

    def teacher_stage(stage, now):
        return forward_stage(stage, images, 1, dp_z, False)(place, now, *teacher_pair)

    now = own(out_grad)
    back = None
    for stage in range(stages - 1, -1, -1):
        if stage == 2:
            x_in, _ = lax.optimization_barrier((x_in, new_dx))
            x_pair = trade(x_in)
            now, x_pair = lax.optimization_barrier((now, x_pair))
            x_all = jnp.concatenate(ring(jnp.stack(x_pair), "x"), axis=0)
        if stage == 1:
            teacher_pair = (teacher_w, swap(teacher_w))
        if stage == 0:
            x_late, _ = lax.optimization_barrier((x_all, new_dx))
            teacher_now, _ = lax.optimization_barrier((own(teacher_in), new_dx))
            left = column_rows(images, group, dp_z, dp_x)(place, x_late)
            teacher_out = teacher_stage(0, teacher_now)
            now, left, teacher_out = lax.optimization_barrier((now, left, teacher_out))
        new_dx, new_d = backward_stage(stage, images)(place, now, *kept[stage][2], weights)
        back = pick(stage, (new_dx, new_d), back)
        if stage > 0:
            sent = new_dx[0]
            if stage == 2:
                sent, teacher_w = lax.optimization_barrier((sent, teacher_w))
            now = lax.ppermute(sent, "y", [(stage, stage - 1)])
    dx, d_mixed = back

    acts = teacher_out
    d_mixed, teacher_now = lax.optimization_barrier((d_mixed, up(teacher_out[1], 0)))
    teacher_out = teacher_stage(1, teacher_now)

    def after_teacher(below, above):
        nonlocal teacher_out
        below, above, teacher_out = lax.optimization_barrier((below, above, teacher_out))
        return below, above

    d_pieces = ring(jnp.stack(trade((d_mixed[0], d_mixed[1]))), "x", after_teacher)
    teacher_now = up(teacher_out[1], 1)
    d_pieces, teacher_now = lax.optimization_barrier((d_pieces, teacher_now))
    blocks = weight_grad(images, dp_z, dp_x)(place, left, *d_pieces)
    shard = lax.psum_scatter(blocks, "z", scatter_dimension=0, tiled=True)
    grad = shard.astype(f32).reshape(1, -1)
    teacher_new = ema_keep * teacher_params + (1.0 - ema_keep) * (student_params - step_rate * grad)

    for stage in range(1, stages):
        if stage > 1:
            teacher_out = teacher_stage(stage, teacher_now if stage == 2 else up(teacher_out[1], stage - 1))
        acts = pick(stage, teacher_out, acts)

    return placed(acts), placed((dx[0], dx[1])), grad, teacher_new


def solution(mesh):
    grid = Mesh(mesh.devices.reshape(4, 2, 8, 4), ("y", "core", "z", "x"))
    seg = ("y", "core")
    dp = ("z", "x")
    image_spec = P(None, dp, None, None, None)
    return jax.shard_map(
        per_device,
        mesh=grid,
        in_specs=(image_spec, image_spec, image_spec, P(seg, dp), P(seg, dp)),
        out_specs=(
            P(seg, None, dp, None, None, None),
            P(seg, None, dp, None, None, None),
            P(seg, dp),
            P(seg, dp),
        ),
        check_vma=False,
    )
```
